32 devices in a mesh: grp: 2 (over x), ctx: 16 (over z, y, core).
Axes of the slice: x: 2, y: 2, z: 4, core: 2. Of those that a mesh axis runs over, the one named last changes fastest.
Arguments:
- queries: bfloat16 [960, 4096], P(None, ('grp', 'ctx')), parts along dimension 1, may hold values from -6 to 6
- key_rows: bfloat16 [960, 4096], P(None, ('grp', 'ctx')), parts along dimension 1, may hold values from -6 to 6
- value_rows: bfloat16 [960, 4096], P(None, ('grp', 'ctx')), parts along dimension 1, may hold values from -6 to 6
- short_taps: float32 [3, 960, 7], replicated, may hold values from -2 to 2
- long_filter: bfloat16 [960, 2048], P('ctx'), may hold values from -0.125 to 0.125
Outputs:
- mixed: bfloat16 [960, 4096], P(None, ('grp', 'ctx')), parts along dimension 1
The draws below stay inside these ranges and needn't reach their ends.
There are 2 independent parts, one for each index of `grp`. The reference program is written for one: setup_inputs(seed, part) draws one part's arguments, and reference() takes and returns one part's arrays. A program takes and returns all parts, laid end to end along the dimension named above; an argument that names none is the same for every part. Nothing has to cross between parts.
All inputs are finite; a program needn't handle non-finite values.
Results may differ from the reference program's by a relative error of at most 0.0057.
Values may be sent and summed in bfloat16 or wider, within the bound.
A program may use at most 64 MiB of HBM per device.

```python
import jax
import jax.numpy as jnp

D = 960
TAPS = 7
SEQ = 2048


def block_scale(stream_key, shape, shards, least, top_value):
    loudness = 1.0
    for axis_at, parts in shards:
        steps = jax.random.uniform(jax.random.fold_in(jax.random.fold_in(stream_key, 6), axis_at), (parts,), jnp.float32, least / len(shards), top_value / len(shards))
        loudness = loudness * jnp.repeat(jnp.exp(steps), shape[axis_at] // parts).reshape((-1,) + (1,) * (len(shape) - 1 - axis_at))
    return loudness


def bell_draw(own_key, extent, scale, limit, split=(), dtype=jnp.bfloat16):
    drawn = scale * jax.random.normal(own_key, extent, jnp.float32)
    if split:
        drawn = drawn * block_scale(own_key, extent, split, -0.22, 0.18)
    return jnp.clip(drawn, -limit, limit).astype(dtype)


def setup_inputs(seed: int = 0, part: int = 0) -> dict:
    key_of = jax.random.split(jax.random.key(seed), 6)
    part_splits = jax.random.split(jax.random.fold_in(key_of[5], part), 6)
    queries = bell_draw(part_splits[0], (D, SEQ), 1.0, 6.0, ((1, 16),))
    key_rows = bell_draw(part_splits[1], (D, SEQ), 1.0, 6.0, ((1, 16),))
    value_rows = bell_draw(part_splits[2], (D, SEQ), 1.0, 6.0, ((1, 16),))
    short_taps = bell_draw(key_of[3], (3, D, TAPS), TAPS ** -0.5, 2.0, (), jnp.float32)
    long_filter = bell_draw(key_of[4], (D, SEQ), SEQ ** -0.5, 0.125, ((0, 16),))
    return dict(queries=queries, key_rows=key_rows, value_rows=value_rows, short_taps=short_taps, long_filter=long_filter)


def short_conv(rows, taps):
    length = rows.shape[1]
    padded = jnp.pad(rows.astype(jnp.float32), ((0, 0), (TAPS - 1, TAPS - 1)))
    mirrored = taps[::-1, :]
    causal = jnp.zeros(rows.shape, jnp.float32)
    anticausal = jnp.zeros(rows.shape, jnp.float32)
    for offset in range(TAPS):
        begin = TAPS - 1 - offset
        causal = causal + taps[:, offset, None] * padded[:, begin:begin + length]
        later = TAPS - 1 + offset
        anticausal = anticausal + mirrored[:, offset, None] * padded[:, later:later + length]
    return causal, anticausal


def reference(queries, key_rows, value_rows, short_taps, long_filter):
    query_fwd, query_bwd = short_conv(queries, short_taps[0])
    key_fwd, key_bwd = short_conv(key_rows, short_taps[1])
    value_fwd, value_bwd = short_conv(value_rows, short_taps[2])
    product_a = (key_fwd * value_fwd).astype(jnp.bfloat16)
    product_b = (key_bwd * value_bwd).astype(jnp.bfloat16)
    padded_len = 2 * SEQ
    filter_spec = jnp.fft.rfft(long_filter.astype(jnp.float32), n=padded_len, axis=1)
    spec_a = jnp.fft.rfft(product_a.astype(jnp.float32), n=padded_len, axis=1)
    mixed_a = jnp.fft.irfft(filter_spec * spec_a, n=padded_len, axis=1)[:, :SEQ]
    mixed_a = mixed_a.astype(jnp.float32).astype(jnp.bfloat16)
    spec_b = jnp.fft.rfft(product_b.astype(jnp.float32), n=padded_len, axis=1)
    mixed_b = jnp.fft.irfft(jnp.conj(filter_spec[::-1]) * spec_b, n=padded_len, axis=1)[:, :SEQ]
    mixed_b = mixed_b.astype(jnp.float32).astype(jnp.bfloat16)
    result = query_fwd * mixed_a.astype(jnp.float32) + query_bwd * mixed_b.astype(jnp.float32)
    return result.astype(jnp.bfloat16)
```

```python
import functools

import jax
import jax.numpy as jnp
from jax import lax
from jax.experimental import pallas as pl
from jax.experimental.pallas import tpu as pltpu
from jax.sharding import PartitionSpec as P

TAPS = 7
LANES = 128
F32 = jnp.float32
BF16 = jnp.bfloat16


def dims_of(cblk):
    cpad = -(-cblk // 16) * 16
    low = (cpad - cblk) // 2
    rows = 32 if cpad % 32 == 0 and 2 * low + cblk == cpad else cpad
    return cpad, low, rows


def unit(flip):
    i = lax.broadcasted_iota(jnp.int32, (LANES, LANES), 0)
    j = lax.broadcasted_iota(jnp.int32, (LANES, LANES), 1)
    j = LANES - 1 - j if flip else j
    return (i == j).astype(F32).astype(BF16)


def to_time_major(mat, x):
    return lax.dot_general(mat, x, (((1,), (1,)), ((), ())), preferred_element_type=F32)


def to_channel_major(x, mat):
    return lax.dot_general(x, mat, (((0,), (0,)), ((), ())), preferred_element_type=F32)


def short_sum(xs, taps, way, which, lanes):
    total = None
    for j in range(TAPS):
        start = 8 - j if way == 0 else 8 + j
        term = taps[way, which, j : j + 1, lanes] * xs[which, start : start + LANES, lanes]
        total = term if total is None else total + term
    return total


def kernel(
    n, cblk, x_ref, taps, filt, out,
    xs, qmix, snd, rcv, osnd, orcv, h32, xfa, xfb, ya, yb, toep, lhs,
    hs_sem, hr_sem, s_sem, r_sem, os_sem, or_sem,
):
    cpad, low, rows = dims_of(cblk)
    nch = cpad // rows
    cp = n * cpad
    me = lax.axis_index("ctx")
    groups = cp // LANES
    per = LANES // cpad

    barrier = pltpu.get_barrier_semaphore()

    def greet(o, carry):
        pl.semaphore_signal(barrier, inc=1, device_id={"ctx": lax.rem(me + o, n)})
        return carry

    lax.fori_loop(1, n, greet, 0)

    eye = unit(False)
    flip = unit(True)
    for a in range(3):
        for g in range(groups):
            ls = slice(g * LANES, (g + 1) * LANES)
            xs[a, 8 : 8 + LANES, ls] = to_time_major(eye, x_ref[a, ls, :])

    pl.semaphore_wait(barrier, n - 1)

    def halo(a, up):
        if up:
            return pltpu.make_async_remote_copy(
                src_ref=xs.at[a, pl.ds(LANES, 8)], dst_ref=xs.at[a, pl.ds(0, 8)],
                send_sem=hs_sem.at[0, a], recv_sem=hr_sem.at[0, a],
                device_id={"ctx": lax.rem(me + 1, n)},
            )
        return pltpu.make_async_remote_copy(
            src_ref=xs.at[a, pl.ds(8, 8)], dst_ref=xs.at[a, pl.ds(8 + LANES, 8)],
            send_sem=hs_sem.at[1, a], recv_sem=hr_sem.at[1, a],
            device_id={"ctx": lax.rem(me + n - 1, n)},
        )

    @pl.when(me < n - 1)
    def _():
        for a in (1, 2, 0):
            halo(a, True).start()

    @pl.when(me > 0)
    def _():
        for a in (1, 2, 0):
            halo(a, False).start()

    @pl.when(me == 0)
    def _():
        xs[:, 0:8, :] = jnp.zeros((3, 8, cp), F32)

    @pl.when(me == n - 1)
    def _():
        xs[:, 8 + LANES : 16 + LANES, :] = jnp.zeros((3, 8, cp), F32)

    for d in range(n):
        h32[d] = filt[:, d * LANES : (d + 1) * LANES].astype(F32)
    xfa[0 : n * rows, :] = jnp.zeros((n * rows, LANES), F32)
    xfb[0 : n * rows, :] = jnp.zeros((n * rows, LANES), F32)

    def halo_wait(arrays):
        @pl.when(me > 0)
        def _():
            for a in arrays:
                halo(a, True).wait_recv()

        @pl.when(me < n - 1)
        def _():
            for a in arrays:
                halo(a, False).wait_recv()

    halo_wait((1, 2))
    for g in range(groups):
        ls = slice(g * LANES, (g + 1) * LANES)
        pa = (short_sum(xs, taps, 0, 1, ls) * short_sum(xs, taps, 0, 2, ls)).astype(BF16)
        pb = (short_sum(xs, taps, 1, 1, ls) * short_sum(xs, taps, 1, 2, ls)).astype(BF16)
        pa = to_channel_major(pa, eye).astype(BF16)
        pb = to_channel_major(pb, flip).astype(BF16)
        for s in range(per):
            block = g * per + s
            for m in range(nch):
                part = slice(s * cpad + m * rows, s * cpad + (m + 1) * rows)
                snd[m, block, 0] = pa[part]
                snd[nch - 1 - m, n - 1 - block, 1] = pb[part]

    def data_copy(m, dest, slot):
        return pltpu.make_async_remote_copy(
            src_ref=snd.at[m, dest], dst_ref=rcv.at[m, slot],
            send_sem=s_sem.at[m, dest], recv_sem=r_sem.at[m, slot],
            device_id={"ctx": dest},
        )

    def back_copy(m, dest, slot):
        return pltpu.make_async_remote_copy(
            src_ref=osnd.at[m, dest], dst_ref=orcv.at[m, slot],
            send_sem=os_sem.at[m, dest], recv_sem=or_sem.at[m, slot],
            device_id={"ctx": dest},
        )

    def each_peer(act):
        def step(o, carry):
            act(lax.rem(me + o, n))
            return carry

        lax.fori_loop(1, n, step, 0)

    for m in range(nch):
        each_peer(lambda peer: data_copy(m, peer, me).start())

    halo_wait((0,))
    for g in range(groups):
        ls = slice(g * LANES, (g + 1) * LANES)
        qmix[0, :, ls] = short_sum(xs, taps, 0, 0, ls)
        qmix[1, :, ls] = short_sum(xs, taps, 1, 0, ls)

    row_id = lax.broadcasted_iota(jnp.int32, (LANES, LANES), 0)
    col_id = lax.broadcasted_iota(jnp.int32, (LANES, LANES), 1)
    causal = col_id >= row_id

    for m in range(nch):
        each_peer(lambda peer: data_copy(m, me, peer).wait_recv())
        rcv[m, me] = snd[m, me]

        def widen(src, carry):
            at = pl.multiple_of((n + src) * rows, rows)
            xfa[pl.ds(at, rows), :] = rcv[m, src, 0].astype(F32)
            at = pl.multiple_of((n + n - 1 - src) * rows, rows)
            xfb[pl.ds(at, rows), :] = rcv[m, src, 1].astype(F32)
            return carry

        lax.fori_loop(0, n, widen, 0, unroll=4)

        first = max(m * rows, low)
        last = min((m + 1) * rows, low + cblk)

        def channel(p, carry):
            row_a = p - m * rows
            row_b = 2 * low + cblk - 1 - p - (nch - 1 - m) * rows
            row_h = p - low

            def fill(d, before):
                at = d * LANES
                if not isinstance(d, int):
                    at = pl.multiple_of(at, LANES)
                line = h32[d, pl.ds(row_h, 1), :]
                turned = pltpu.roll(
                    jnp.broadcast_to(line, (LANES, LANES)), 0, 1, stride=1, stride_axis=0
                )
                toep[pl.ds(at, LANES), :] = jnp.where(causal, turned, before).astype(BF16)
                xa = xfa[pl.ds((n - d) * rows + row_a, n, stride=rows), :]
                xb = xfb[pl.ds((n - d) * rows + row_b, n, stride=rows), :]
                lhs[:, pl.ds(at, LANES)] = jnp.concatenate([xa, xb], axis=0).astype(BF16)
                return turned

            start = jnp.zeros((LANES, LANES), F32)
            if n <= 16:
                for d in range(n):
                    start = fill(d, start)
            else:
                lax.fori_loop(0, n, fill, start)
            y = jnp.dot(lhs[...], toep[...], preferred_element_type=F32)
            ya[pl.ds(row_a, n, stride=rows), :] = y[:n]
            yb[pl.ds(row_b, n, stride=rows), :] = y[n:]
            return carry

        lax.fori_loop(first, last, channel, 0)

        def narrow(dest, carry):
            at = pl.multiple_of(dest * rows, rows)
            osnd[m, dest, 0] = ya[pl.ds(at, rows), :].astype(BF16)
            at = pl.multiple_of((n - 1 - dest) * rows, rows)
            osnd[m, dest, 1] = yb[pl.ds(at, rows), :].astype(BF16)
            return carry

        lax.fori_loop(0, n, narrow, 0, unroll=4)
        each_peer(lambda peer: back_copy(m, peer, me).start())
        orcv[m, me] = osnd[m, me]

    for m in range(nch):
        each_peer(lambda peer: back_copy(m, me, peer).wait_recv())

    for g in range(groups):
        ls = slice(g * LANES, (g + 1) * LANES)
        blocks = [g * per + s for s in range(per)]
        ma = jnp.concatenate([orcv[m, b, 0] for b in blocks for m in range(nch)], axis=0)
        mb = jnp.concatenate(
            [orcv[nch - 1 - m, n - 1 - b, 1] for b in blocks for m in range(nch)], axis=0
        )
        mixed = qmix[0, :, ls] * to_time_major(eye, ma) + qmix[1, :, ls] * to_time_major(flip, mb)
        out[ls, :] = to_channel_major(mixed.astype(BF16), eye).astype(BF16)

    for m in range(nch):
        each_peer(lambda peer: data_copy(m, peer, me).wait_send())
        each_peer(lambda peer: back_copy(m, peer, me).wait_send())

    @pl.when(me < n - 1)
    def _():
        for a in range(3):
            halo(a, True).wait_send()

    @pl.when(me > 0)
    def _():
        for a in range(3):
            halo(a, False).wait_send()


def on_device(queries, key_rows, value_rows, short_taps, long_filter):
    n = lax.axis_size("ctx")
    channels, tokens = queries.shape
    cblk, length = long_filter.shape
    cpad, low, rows = dims_of(cblk)
    nch = cpad // rows
    cp = n * cpad
    pad = ((0, 0), (0, 0), (low, cpad - cblk - low), (0, 0))
    x = jnp.stack([queries, key_rows, value_rows]).reshape(3, n, cblk, tokens)
    x = jnp.pad(x, pad).reshape(3, cp, tokens)
    taps = jnp.stack([short_taps, short_taps[:, ::-1, :]]).reshape(6, n, cblk, TAPS)
    taps = jnp.pad(taps, pad).reshape(2, 3, cp, TAPS)
    taps = jnp.pad(jnp.swapaxes(taps, 2, 3), ((0, 0), (0, 0), (0, 1), (0, 0)))
    vmem = pl.BlockSpec(memory_space=pltpu.VMEM)
    dma = pltpu.SemaphoreType.DMA
    mixed = pl.pallas_call(
        functools.partial(kernel, n, cblk),
        out_shape=jax.ShapeDtypeStruct((cp, tokens), BF16),
        in_specs=[vmem] * 3,
        out_specs=vmem,
        scratch_shapes=[
            pltpu.VMEM((3, LANES + 16, cp), F32),
            pltpu.VMEM((2, LANES, cp), F32),
            pltpu.VMEM((nch, n, 2, rows, LANES), BF16),
            pltpu.VMEM((nch, n, 2, rows, LANES), BF16),
            pltpu.VMEM((nch, n, 2, rows, LANES), BF16),
            pltpu.VMEM((nch, n, 2, rows, LANES), BF16),
            pltpu.VMEM((n, cblk, LANES), F32),
            pltpu.VMEM((2 * n * rows, LANES), F32),
            pltpu.VMEM((2 * n * rows, LANES), F32),
            pltpu.VMEM((n * rows, LANES), F32),
            pltpu.VMEM((n * rows, LANES), F32),
            pltpu.VMEM((length, LANES), BF16),
            pltpu.VMEM((2 * n, length), BF16),
            dma((2, 3)),
            dma((2, 3)),
            dma((nch, n)),
            dma((nch, n)),
            dma((nch, n)),
            dma((nch, n)),
        ],
        compiler_params=pltpu.CompilerParams(
            collective_id=0, has_side_effects=True, vmem_limit_bytes=48 * 1024 * 1024
        ),
    )(x, taps, long_filter)
    mixed = mixed.reshape(n, cpad, tokens)[:, low : low + cblk]
    return mixed.reshape(channels, tokens)


def solution(mesh):
    placed = (
        P(None, ("grp", "ctx")),
        P(None, ("grp", "ctx")),
        P(None, ("grp", "ctx")),
        P(),
        P("ctx", None),
    )
    return jax.shard_map(
        on_device, mesh=mesh, in_specs=placed, out_specs=P(None, ("grp", "ctx")), check_vma=False
    )
```

```python
import functools

import jax
import jax.numpy as jnp
from jax import lax
from jax.experimental import pallas as pl
from jax.experimental.pallas import tpu as pltpu
from jax.sharding import PartitionSpec as P

TAPS = 7
LANES = 128
F32 = jnp.float32
BF16 = jnp.bfloat16


def dims_of(cblk):
    cpad = -(-cblk // 16) * 16
    low = (cpad - cblk) // 2
    rows = 32 if cpad % 32 == 0 and 2 * low + cblk == cpad else cpad
    return cpad, low, rows


def unit(flip):
    i = lax.broadcasted_iota(jnp.int32, (LANES, LANES), 0)
    j = lax.broadcasted_iota(jnp.int32, (LANES, LANES), 1)
    j = LANES - 1 - j if flip else j
    return (i == j).astype(F32).astype(BF16)


def to_time_major(mat, x):
    return lax.dot_general(mat, x, (((1,), (1,)), ((), ())), preferred_element_type=F32)


def to_channel_major(x, mat):
    return lax.dot_general(x, mat, (((0,), (0,)), ((), ())), preferred_element_type=F32)


def short_sum(xs, taps, way, which, lanes):
    total = None
    for j in range(TAPS):
        start = 8 - j if way == 0 else 8 + j
        term = taps[way, which, j : j + 1, lanes] * xs[which, start : start + LANES, lanes]
        total = term if total is None else total + term
    return total


def kernel(
    n, cblk, x_ref, taps, filt, out,
    xs, qmix, snd, rcv, osnd, orcv, h32, xfa, xfb, ya, yb, toep0, toep1, lhs0, lhs1, xc0, xc1,
    hs_sem, hr_sem, s_sem, r_sem, os_sem, or_sem,
):
    cpad, low, rows = dims_of(cblk)
    nch = cpad // rows
    cp = n * cpad
    me = lax.axis_index("ctx")
    toep, lhs, xc = (toep0, toep1), (lhs0, lhs1), (xc0, xc1)
    groups = cp // LANES
    per = LANES // cpad

    barrier = pltpu.get_barrier_semaphore()

    def greet(o, carry):
        pl.semaphore_signal(barrier, inc=1, device_id={"ctx": lax.rem(me + o, n)})
        return carry

    lax.fori_loop(1, n, greet, 0)

    eye = unit(False)
    flip = unit(True)
    for a in range(3):
        for g in range(groups):
            ls = slice(g * LANES, (g + 1) * LANES)
            xs[a, 8 : 8 + LANES, ls] = to_time_major(eye, x_ref[a, ls, :])

    pl.semaphore_wait(barrier, n - 1)

    def halo(a, up):
        if up:
            return pltpu.make_async_remote_copy(
                src_ref=xs.at[a, pl.ds(LANES, 8)], dst_ref=xs.at[a, pl.ds(0, 8)],
                send_sem=hs_sem.at[0, a], recv_sem=hr_sem.at[0, a],
                device_id={"ctx": lax.rem(me + 1, n)},
            )
        return pltpu.make_async_remote_copy(
            src_ref=xs.at[a, pl.ds(8, 8)], dst_ref=xs.at[a, pl.ds(8 + LANES, 8)],
            send_sem=hs_sem.at[1, a], recv_sem=hr_sem.at[1, a],
            device_id={"ctx": lax.rem(me + n - 1, n)},
        )

    @pl.when(me < n - 1)
    def _():
        for a in (1, 2, 0):
            halo(a, True).start()

    @pl.when(me > 0)
    def _():
        for a in (1, 2, 0):
            halo(a, False).start()

    @pl.when(me == 0)
    def _():
        xs[:, 0:8, :] = jnp.zeros((3, 8, cp), F32)

    @pl.when(me == n - 1)
    def _():
        xs[:, 8 + LANES : 16 + LANES, :] = jnp.zeros((3, 8, cp), F32)

    for d in range(n):
        h32[d] = filt[:, d * LANES : (d + 1) * LANES].astype(F32)
    for half in range(2):
        xc[half][:, 0:n, :] = jnp.zeros((2, n, LANES), F32)

    def halo_wait(arrays):
        @pl.when(me > 0)
        def _():
            for a in arrays:
                halo(a, True).wait_recv()

        @pl.when(me < n - 1)
        def _():
            for a in arrays:
                halo(a, False).wait_recv()

    halo_wait((1, 2))
    for g in range(groups):
        ls = slice(g * LANES, (g + 1) * LANES)
        pa = (short_sum(xs, taps, 0, 1, ls) * short_sum(xs, taps, 0, 2, ls)).astype(BF16)
        pb = (short_sum(xs, taps, 1, 1, ls) * short_sum(xs, taps, 1, 2, ls)).astype(BF16)
        pa = to_channel_major(pa, eye).astype(BF16)
        pb = to_channel_major(pb, flip).astype(BF16)
        for s in range(per):
            block = g * per + s
            for m in range(nch):
                part = slice(s * cpad + m * rows, s * cpad + (m + 1) * rows)
                snd[m, block, 0] = pa[part]
                snd[nch - 1 - m, n - 1 - block, 1] = pb[part]

    def data_copy(m, dest, slot):
        return pltpu.make_async_remote_copy(
            src_ref=snd.at[m, dest], dst_ref=rcv.at[m, slot],
            send_sem=s_sem.at[m, dest], recv_sem=r_sem.at[m, slot],
            device_id={"ctx": dest},
        )

    def back_copy(m, dest, slot):
        return pltpu.make_async_remote_copy(
            src_ref=osnd.at[m, dest], dst_ref=orcv.at[m, slot],
            send_sem=os_sem.at[m, dest], recv_sem=or_sem.at[m, slot],
            device_id={"ctx": dest},
        )

    def each_peer(act):
        def step(o, carry):
            act(lax.rem(me + o, n))
            return carry

        lax.fori_loop(1, n, step, 0)

    for m in range(nch):
        each_peer(lambda peer: data_copy(m, peer, me).start())

    halo_wait((0,))
    for g in range(groups):
        ls = slice(g * LANES, (g + 1) * LANES)
        qmix[0, :, ls] = short_sum(xs, taps, 0, 0, ls)
        qmix[1, :, ls] = short_sum(xs, taps, 1, 0, ls)

    row_id = lax.broadcasted_iota(jnp.int32, (LANES, LANES), 0)
    col_id = lax.broadcasted_iota(jnp.int32, (LANES, LANES), 1)
    causal = col_id >= row_id

    for m in range(nch):
        each_peer(lambda peer: data_copy(m, me, peer).wait_recv())
        rcv[m, me] = snd[m, me]

        def widen(src, carry):
            at = pl.multiple_of(src * rows, rows)
            xfa[pl.ds(at, rows), :] = rcv[m, src, 0].astype(F32)
            at = pl.multiple_of((n - 1 - src) * rows, rows)
            xfb[pl.ds(at, rows), :] = rcv[m, src, 1].astype(F32)
            return carry

        lax.fori_loop(0, n, widen, 0, unroll=4)

        first = max(m * rows, low)
        last = min((m + 1) * rows, low + cblk)

        count = last - first

        def build(p, half):
            row_a = p - m * rows
            row_b = 2 * low + cblk - 1 - p - (nch - 1 - m) * rows
            row_h = p - low
            line_x = xc[half]
            line_x[0, n : 2 * n, :] = xfa[pl.ds(row_a, n, stride=rows), :]
            line_x[1, n : 2 * n, :] = xfb[pl.ds(row_b, n, stride=rows), :]

            def fill(d, before):
                at = d * LANES
                if not isinstance(d, int):
                    at = pl.multiple_of(at, LANES)
                line = h32[d, pl.ds(row_h, 1), :]
                turned = pltpu.roll(
                    jnp.broadcast_to(line, (LANES, LANES)), 0, 1, stride=1, stride_axis=0
                )
                toep[half][pl.ds(at, LANES), :] = jnp.where(causal, turned, before).astype(BF16)
                xa = line_x[0, pl.ds(n - d, n), :]
                xb = line_x[1, pl.ds(n - d, n), :]
                lhs[half][:, pl.ds(at, LANES)] = jnp.concatenate([xa, xb], axis=0).astype(BF16)
                return turned

            start = jnp.zeros((LANES, LANES), F32)
            if n <= 16:
                for d in range(n):
                    start = fill(d, start)
            else:
                lax.fori_loop(0, n, fill, start)

        def apply(p, half):
            row_a = p - m * rows
            row_b = 2 * low + cblk - 1 - p - (nch - 1 - m) * rows
            y = jnp.dot(lhs[half][...], toep[half][...], preferred_element_type=F32)
            ya[pl.ds(row_a, n, stride=rows), :] = y[:n]
            yb[pl.ds(row_b, n, stride=rows), :] = y[n:]

        def pair(i, carry):
            build(first + 2 * i + 1, 1)
            apply(first + 2 * i, 0)
            build(first + lax.rem(2 * i + 2, count), 0)
            apply(first + 2 * i + 1, 1)
            return carry

        build(first, 0)
        lax.fori_loop(0, count // 2, pair, 0)
        if count % 2:
            apply(last - 1, 0)

        def narrow(dest, carry):
            at = pl.multiple_of(dest * rows, rows)
            osnd[m, dest, 0] = ya[pl.ds(at, rows), :].astype(BF16)
            at = pl.multiple_of((n - 1 - dest) * rows, rows)
            osnd[m, dest, 1] = yb[pl.ds(at, rows), :].astype(BF16)
            return carry

        lax.fori_loop(0, n, narrow, 0, unroll=4)
        each_peer(lambda peer: back_copy(m, peer, me).start())
        orcv[m, me] = osnd[m, me]

    for m in range(nch):
        each_peer(lambda peer: back_copy(m, me, peer).wait_recv())

    for g in range(groups):
        ls = slice(g * LANES, (g + 1) * LANES)
        blocks = [g * per + s for s in range(per)]
        ma = jnp.concatenate([orcv[m, b, 0] for b in blocks for m in range(nch)], axis=0)
        mb = jnp.concatenate(
            [orcv[nch - 1 - m, n - 1 - b, 1] for b in blocks for m in range(nch)], axis=0
        )
        mixed = qmix[0, :, ls] * to_time_major(eye, ma) + qmix[1, :, ls] * to_time_major(flip, mb)
        out[ls, :] = to_channel_major(mixed.astype(BF16), eye).astype(BF16)

    for m in range(nch):
        each_peer(lambda peer: data_copy(m, peer, me).wait_send())
        each_peer(lambda peer: back_copy(m, peer, me).wait_send())

    @pl.when(me < n - 1)
    def _():
        for a in range(3):
            halo(a, True).wait_send()

    @pl.when(me > 0)
    def _():
        for a in range(3):
            halo(a, False).wait_send()


def on_device(queries, key_rows, value_rows, short_taps, long_filter):
    n = lax.axis_size("ctx")
    channels, tokens = queries.shape
    cblk, length = long_filter.shape
    cpad, low, rows = dims_of(cblk)
    nch = cpad // rows
    cp = n * cpad
    pad = ((0, 0), (0, 0), (low, cpad - cblk - low), (0, 0))
    x = jnp.stack([queries, key_rows, value_rows]).reshape(3, n, cblk, tokens)
    x = jnp.pad(x, pad).reshape(3, cp, tokens)
    taps = jnp.stack([short_taps, short_taps[:, ::-1, :]]).reshape(6, n, cblk, TAPS)
    taps = jnp.pad(taps, pad).reshape(2, 3, cp, TAPS)
    taps = jnp.pad(jnp.swapaxes(taps, 2, 3), ((0, 0), (0, 0), (0, 1), (0, 0)))
    vmem = pl.BlockSpec(memory_space=pltpu.VMEM)
    dma = pltpu.SemaphoreType.DMA
    mixed = pl.pallas_call(
        functools.partial(kernel, n, cblk),
        out_shape=jax.ShapeDtypeStruct((cp, tokens), BF16),
        in_specs=[vmem] * 3,
        out_specs=vmem,
        scratch_shapes=[
            pltpu.VMEM((3, LANES + 16, cp), F32),
            pltpu.VMEM((2, LANES, cp), F32),
            pltpu.VMEM((nch, n, 2, rows, LANES), BF16),
            pltpu.VMEM((nch, n, 2, rows, LANES), BF16),
            pltpu.VMEM((nch, n, 2, rows, LANES), BF16),
            pltpu.VMEM((nch, n, 2, rows, LANES), BF16),
            pltpu.VMEM((n, cblk, LANES), F32),
            pltpu.VMEM((n * rows, LANES), F32),
            pltpu.VMEM((n * rows, LANES), F32),
            pltpu.VMEM((n * rows, LANES), F32),
            pltpu.VMEM((n * rows, LANES), F32),
            pltpu.VMEM((length, LANES), BF16),
            pltpu.VMEM((length, LANES), BF16),
            pltpu.VMEM((2 * n, length), BF16),
            pltpu.VMEM((2 * n, length), BF16),
            pltpu.VMEM((2, 2 * n, LANES), F32),
            pltpu.VMEM((2, 2 * n, LANES), F32),
            dma((2, 3)),
            dma((2, 3)),
            dma((nch, n)),
            dma((nch, n)),
            dma((nch, n)),
            dma((nch, n)),
        ],
        compiler_params=pltpu.CompilerParams(
            collective_id=0, has_side_effects=True, vmem_limit_bytes=48 * 1024 * 1024
        ),
    )(x, taps, long_filter)
    mixed = mixed.reshape(n, cpad, tokens)[:, low : low + cblk]
    return mixed.reshape(channels, tokens)


def solution(mesh):
    placed = (
        P(None, ("grp", "ctx")),
        P(None, ("grp", "ctx")),
        P(None, ("grp", "ctx")),
        P(),
        P("ctx", None),
    )
    return jax.shard_map(
        on_device, mesh=mesh, in_specs=placed, out_specs=P(None, ("grp", "ctx")), check_vma=False
    )
```

```python
import functools

import jax
import jax.numpy as jnp
from jax import lax
from jax.experimental import pallas as pl
from jax.experimental.pallas import tpu as pltpu
from jax.sharding import PartitionSpec as P

TAPS = 7
LANES = 128
F32 = jnp.float32
BF16 = jnp.bfloat16


def dims_of(cblk):
    cpad = -(-cblk // 16) * 16
    low = (cpad - cblk) // 2
    rows = 16 if cpad % 16 == 0 and 2 * low + cblk == cpad else cpad
    return cpad, low, rows


def unit(flip):
    i = lax.broadcasted_iota(jnp.int32, (LANES, LANES), 0)
    j = lax.broadcasted_iota(jnp.int32, (LANES, LANES), 1)
    j = LANES - 1 - j if flip else j
    return (i == j).astype(F32).astype(BF16)


def to_time_major(mat, x):
    return lax.dot_general(mat, x, (((1,), (1,)), ((), ())), preferred_element_type=F32)


def to_channel_major(x, mat):
    return lax.dot_general(x, mat, (((0,), (0,)), ((), ())), preferred_element_type=F32)


def short_sum(xs, taps, way, which, lanes):
    total = None
    for j in range(TAPS):
        start = 8 - j if way == 0 else 8 + j
        term = taps[way, which, j : j + 1, lanes] * xs[which, start : start + LANES, lanes]
        total = term if total is None else total + term
    return total


def kernel(
    n, cblk, q_hbm, k_hbm, v_hbm, taps_hbm, filt_hbm, out,
    xin, tin, filt, in_sem, alt, taps, xf, xs, qmix, snd, rcv, osnd, orcv, h32, xfa, xfb, ya, yb, toep0, toep1, lhs0, lhs1, xc0, xc1,
    hs_sem, hr_sem, s_sem, r_sem, os_sem, or_sem,
):
    cpad, low, rows = dims_of(cblk)
    nch = cpad // rows
    cp = n * cpad
    me = lax.axis_index("ctx")
    toep, lhs, xc = (toep0, toep1), (lhs0, lhs1), (xc0, xc1)
    groups = cp // LANES
    per = LANES // cpad

    barrier = pltpu.get_barrier_semaphore()

    def greet(o, carry):
        pl.semaphore_signal(barrier, inc=1, device_id={"ctx": lax.rem(me + o, n)})
        return carry

    lax.fori_loop(1, n, greet, 0)

    loads = [
        pltpu.make_async_copy(src, dst, in_sem.at[i])
        for i, (src, dst) in enumerate((
            (q_hbm, xin.at[0]), (k_hbm, xin.at[1]), (v_hbm, xin.at[2]),
            (taps_hbm, tin), (filt_hbm, filt),
        ))
    ]
    for i in (1, 2, 3, 0, 4):
        loads[i].start()

    eye = unit(False)
    flip = unit(True)
    channels = n * cblk
    held = 8 + channels
    for half in range(2):
        xc[half][:, 0:n, :] = jnp.zeros((2, n, LANES), F32)
    taps[...] = jnp.zeros((2, 3, 8, cp), F32)
    alt[...] = jnp.zeros((3, 8, cp), F32)
    for a in range(3):
        xf[a, 0:8, :] = jnp.zeros((8, LANES), F32)
        xf[a, held : held + 16, :] = jnp.zeros((16, LANES), F32)

    def turn(a):
        loads[a].wait()
        xf[a, 8:held, :] = xin[a].astype(F32)
        for g in range(groups):
            starts = [8 + (g * per + s) * cblk - low for s in range(per)]
            wide = jnp.concatenate([xf[a, i : i + cpad, :] for i in starts], axis=0).astype(BF16)
            xs[a, 8 : 8 + LANES, g * LANES : (g + 1) * LANES] = to_time_major(eye, wide)

    def halo(a, up):
        if up:
            return pltpu.make_async_remote_copy(
                src_ref=xs.at[a, pl.ds(LANES, 8)], dst_ref=xs.at[a, pl.ds(0, 8)],
                send_sem=hs_sem.at[0, a], recv_sem=hr_sem.at[0, a],
                device_id={"ctx": lax.rem(me + 1, n)},
            )
        return pltpu.make_async_remote_copy(
            src_ref=xs.at[a, pl.ds(8, 8)], dst_ref=xs.at[a, pl.ds(8 + LANES, 8)],
            send_sem=hs_sem.at[1, a], recv_sem=hr_sem.at[1, a],
            device_id={"ctx": lax.rem(me + n - 1, n)},
        )

    @pl.when(me == 0)
    def _():
        xs[:, 0:8, :] = jnp.zeros((3, 8, cp), F32)

    @pl.when(me == n - 1)
    def _():
        xs[:, 8 + LANES : 16 + LANES, :] = jnp.zeros((3, 8, cp), F32)

    def halo_wait(arrays):
        @pl.when(me > 0)
        def _():
            for a in arrays:
                halo(a, True).wait_recv()

        @pl.when(me < n - 1)
        def _():
            for a in arrays:
                halo(a, False).wait_recv()

    def halo_start(arrays):
        @pl.when(me < n - 1)
        def _():
            for a in arrays:
                halo(a, True).start()

        @pl.when(me > 0)
        def _():
            for a in arrays:
                halo(a, False).start()

    turn(1)
    turn(2)
    pl.semaphore_wait(barrier, n - 1)
    halo_start((1, 2))
    turn(0)
    halo_start((0,))
    loads[3].wait()
    for ref, shift in ((taps.at[0], low), (alt, cpad - cblk - low)):
        for b in range(n):
            base = b * cblk - shift
            lo, hi = max(base, 0), min(base + cpad, channels)
            at = b * cpad + lo - base
            ref[:, 0:TAPS, at : at + hi - lo] = tin[:, :, lo:hi]
    turner = unit(True).astype(F32)
    for g in range(groups):
        source = alt[:, :, cp - (g + 1) * LANES : cp - g * LANES].reshape(24, LANES)
        taps[1, :, :, g * LANES : (g + 1) * LANES] = jnp.dot(
            source, turner, precision=lax.Precision.HIGHEST, preferred_element_type=F32
        ).reshape(3, 8, LANES)
    loads[4].wait()
    for d in range(n):
        h32[d] = filt[:, d * LANES : (d + 1) * LANES].astype(F32)

    halo_wait((1, 2))
    for g in range(groups):
        ls = slice(g * LANES, (g + 1) * LANES)
        pa = (short_sum(xs, taps, 0, 1, ls) * short_sum(xs, taps, 0, 2, ls)).astype(BF16)
        pb = (short_sum(xs, taps, 1, 1, ls) * short_sum(xs, taps, 1, 2, ls)).astype(BF16)
        pa = to_channel_major(pa, eye).astype(BF16)
        pb = to_channel_major(pb, flip).astype(BF16)
        for s in range(per):
            block = g * per + s
            for m in range(nch):
                part = slice(s * cpad + m * rows, s * cpad + (m + 1) * rows)
                snd[m, block, 0] = pa[part]
                snd[nch - 1 - m, n - 1 - block, 1] = pb[part]

    def data_copy(m, dest, slot):
        return pltpu.make_async_remote_copy(
            src_ref=snd.at[m, dest], dst_ref=rcv.at[m, slot],
            send_sem=s_sem.at[m, dest], recv_sem=r_sem.at[m, slot],
            device_id={"ctx": dest},
        )

    def back_copy(m, dest, slot):
        return pltpu.make_async_remote_copy(
            src_ref=osnd.at[m, dest], dst_ref=orcv.at[m, slot],
            send_sem=os_sem.at[m, dest], recv_sem=or_sem.at[m, slot],
            device_id={"ctx": dest},
        )

    def each_peer(act):
        def step(o, carry):
            act(lax.rem(me + o, n))
            return carry

        lax.fori_loop(1, n, step, 0)

    for m in range(nch):
        each_peer(lambda peer: data_copy(m, peer, me).start())

    halo_wait((0,))
    for g in range(groups):
        ls = slice(g * LANES, (g + 1) * LANES)
        qmix[0, :, ls] = short_sum(xs, taps, 0, 0, ls)
        qmix[1, :, ls] = short_sum(xs, taps, 1, 0, ls)

    row_id = lax.broadcasted_iota(jnp.int32, (LANES, LANES), 0)
    col_id = lax.broadcasted_iota(jnp.int32, (LANES, LANES), 1)
    causal = col_id >= row_id

    for m in range(nch):
        each_peer(lambda peer: data_copy(m, me, peer).wait_recv())
        rcv[m, me] = snd[m, me]

        def widen(src, carry):
            at = pl.multiple_of(src * rows, rows)
            xfa[pl.ds(at, rows), :] = rcv[m, src, 0].astype(F32)
            at = pl.multiple_of((n - 1 - src) * rows, rows)
            xfb[pl.ds(at, rows), :] = rcv[m, src, 1].astype(F32)
            return carry

        lax.fori_loop(0, n, widen, 0, unroll=4)

        first = max(m * rows, low)
        last = min((m + 1) * rows, low + cblk)

        count = last - first

        def build(p, half):
            row_a = p - m * rows
            row_b = 2 * low + cblk - 1 - p - (nch - 1 - m) * rows
            row_h = p - low
            line_x = xc[half]
            line_x[0, n : 2 * n, :] = xfa[pl.ds(row_a, n, stride=rows), :]
            line_x[1, n : 2 * n, :] = xfb[pl.ds(row_b, n, stride=rows), :]

            def fill(d, before):
                at = d * LANES
                if not isinstance(d, int):
                    at = pl.multiple_of(at, LANES)
                line = h32[d, pl.ds(row_h, 1), :]
                turned = pltpu.roll(
                    jnp.broadcast_to(line, (LANES, LANES)), 0, 1, stride=1, stride_axis=0
                )
                toep[half][pl.ds(at, LANES), :] = jnp.where(causal, turned, before).astype(BF16)
                xa = line_x[0, pl.ds(n - d, n), :]
                xb = line_x[1, pl.ds(n - d, n), :]
                lhs[half][:, pl.ds(at, LANES)] = jnp.concatenate([xa, xb], axis=0).astype(BF16)
                return turned

            start = jnp.zeros((LANES, LANES), F32)
            if n <= 16:
                for d in range(n):
                    start = fill(d, start)
            else:
                lax.fori_loop(0, n, fill, start)

        def apply(p, half):
            row_a = p - m * rows
            row_b = 2 * low + cblk - 1 - p - (nch - 1 - m) * rows
            y = jnp.dot(lhs[half][...], toep[half][...], preferred_element_type=F32)
            ya[pl.ds(row_a, n, stride=rows), :] = y[:n]
            yb[pl.ds(row_b, n, stride=rows), :] = y[n:]

        def pair(i, carry):
            build(first + 2 * i + 1, 1)
            apply(first + 2 * i, 0)
            build(first + lax.rem(2 * i + 2, count), 0)
            apply(first + 2 * i + 1, 1)
            return carry

        build(first, 0)
        lax.fori_loop(0, count // 2, pair, 0)
        if count % 2:
            apply(last - 1, 0)

        def narrow(dest, carry):
            at = pl.multiple_of(dest * rows, rows)
            osnd[m, dest, 0] = ya[pl.ds(at, rows), :].astype(BF16)
            at = pl.multiple_of((n - 1 - dest) * rows, rows)
            osnd[m, dest, 1] = yb[pl.ds(at, rows), :].astype(BF16)
            return carry

        lax.fori_loop(0, n, narrow, 0, unroll=4)
        each_peer(lambda peer: back_copy(m, peer, me).start())
        orcv[m, me] = osnd[m, me]

    for m in range(nch):
        each_peer(lambda peer: back_copy(m, me, peer).wait_recv())

    for g in range(groups):
        ls = slice(g * LANES, (g + 1) * LANES)
        blocks = [g * per + s for s in range(per)]
        ma = jnp.concatenate([orcv[m, b, 0] for b in blocks for m in range(nch)], axis=0)
        mb = jnp.concatenate(
            [orcv[nch - 1 - m, n - 1 - b, 1] for b in blocks for m in range(nch)], axis=0
        )
        mixed = qmix[0, :, ls] * to_time_major(eye, ma) + qmix[1, :, ls] * to_time_major(flip, mb)
        mixed = to_channel_major(mixed.astype(BF16), eye)
        for s, b in enumerate(blocks):
            part = mixed[s * cpad + low : s * cpad + low + cblk]
            xf[0, 8 + b * cblk : 8 + (b + 1) * cblk, :] = part
    out[...] = xf[0, 8:held, :].astype(BF16)

    for m in range(nch):
        each_peer(lambda peer: data_copy(m, peer, me).wait_send())
        each_peer(lambda peer: back_copy(m, peer, me).wait_send())

    @pl.when(me < n - 1)
    def _():
        for a in range(3):
            halo(a, True).wait_send()

    @pl.when(me > 0)
    def _():
        for a in range(3):
            halo(a, False).wait_send()


def on_device(queries, key_rows, value_rows, short_taps, long_filter):
    n = lax.axis_size("ctx")
    channels, tokens = queries.shape
    cblk, length = long_filter.shape
    cpad, low, rows = dims_of(cblk)
    nch = cpad // rows
    cp = n * cpad
    taps = jnp.swapaxes(short_taps, 1, 2)
    hbm = pl.BlockSpec(memory_space=pltpu.MemorySpace.HBM)
    vmem = pl.BlockSpec(memory_space=pltpu.VMEM)
    dma = pltpu.SemaphoreType.DMA
    return pl.pallas_call(
        functools.partial(kernel, n, cblk),
        out_shape=jax.ShapeDtypeStruct((channels, tokens), BF16),
        in_specs=[hbm] * 5,
        out_specs=vmem,
        scratch_shapes=[
            pltpu.VMEM((3, channels, tokens), BF16),
            pltpu.VMEM((3, TAPS, channels), F32),
            pltpu.VMEM((cblk, length), BF16),
            dma((5,)),
            pltpu.VMEM((3, 8, cp), F32),
            pltpu.VMEM((2, 3, 8, cp), F32),
            pltpu.VMEM((3, channels + 24, LANES), F32),
            pltpu.VMEM((3, LANES + 16, cp), F32),
            pltpu.VMEM((2, LANES, cp), F32),
            pltpu.VMEM((nch, n, 2, rows, LANES), BF16),
            pltpu.VMEM((nch, n, 2, rows, LANES), BF16),
            pltpu.VMEM((nch, n, 2, rows, LANES), BF16),
            pltpu.VMEM((nch, n, 2, rows, LANES), BF16),
            pltpu.VMEM((n, cblk, LANES), F32),
            pltpu.VMEM((n * rows, LANES), F32),
            pltpu.VMEM((n * rows, LANES), F32),
            pltpu.VMEM((n * rows, LANES), F32),
            pltpu.VMEM((n * rows, LANES), F32),
            pltpu.VMEM((length, LANES), BF16),
            pltpu.VMEM((length, LANES), BF16),
            pltpu.VMEM((2 * n, length), BF16),
            pltpu.VMEM((2 * n, length), BF16),
            pltpu.VMEM((2, 2 * n, LANES), F32),
            pltpu.VMEM((2, 2 * n, LANES), F32),
            dma((2, 3)),
            dma((2, 3)),
            dma((nch, n)),
            dma((nch, n)),
            dma((nch, n)),
            dma((nch, n)),
        ],
        compiler_params=pltpu.CompilerParams(
            collective_id=0, has_side_effects=True, vmem_limit_bytes=62 * 1024 * 1024
        ),
    )(queries, key_rows, value_rows, taps, long_filter)


def solution(mesh):
    placed = (
        P(None, ("grp", "ctx")),
        P(None, ("grp", "ctx")),
        P(None, ("grp", "ctx")),
        P(),
        P("ctx", None),
    )
    return jax.shard_map(
        on_device, mesh=mesh, in_specs=placed, out_specs=P(None, ("grp", "ctx")), check_vma=False
    )
```

```python
import functools

import jax
import jax.numpy as jnp
from jax import lax
from jax.experimental import pallas as pl
from jax.experimental.pallas import tpu as pltpu
from jax.sharding import PartitionSpec as P

TAPS = 7
LANES = 128
F32 = jnp.float32
BF16 = jnp.bfloat16


def dims_of(cblk):
    cpad = -(-cblk // 16) * 16
    low = (cpad - cblk) // 2
    rows = 16 if cpad % 16 == 0 and 2 * low + cblk == cpad else cpad
    return cpad, low, rows


def unit(flip):
    i = lax.broadcasted_iota(jnp.int32, (LANES, LANES), 0)
    j = lax.broadcasted_iota(jnp.int32, (LANES, LANES), 1)
    j = LANES - 1 - j if flip else j
    return (i == j).astype(F32).astype(BF16)


def to_time_major(mat, x):
    return lax.dot_general(mat, x, (((1,), (1,)), ((), ())), preferred_element_type=F32)


def to_channel_major(x, mat):
    return lax.dot_general(x, mat, (((0,), (0,)), ((), ())), preferred_element_type=F32)


def short_sum(xs, taps, way, which, lanes):
    total = None
    for j in range(TAPS):
        start = 8 - j if way == 0 else 8 + j
        term = taps[way, which, j : j + 1, lanes] * xs[which, start : start + LANES, lanes]
        total = term if total is None else total + term
    return total


def kernel(
    n, cblk, q_hbm, k_hbm, v_hbm, taps_hbm, filt_hbm, out,
    xin, tin, filt, in_sem, alt, taps, xf, xs, qmix, snd, rcv, osnd, orcv, h32, xfa, xfb, ya, yb, toep0, toep1, lhs0, lhs1, xc0, xc1,
    hs_sem, hr_sem, s_sem, r_sem, os_sem, or_sem,
):
    cpad, low, rows = dims_of(cblk)
    nch = cpad // rows
    cp = n * cpad
    me = lax.axis_index("ctx")
    toep, lhs, xc = (toep0, toep1), (lhs0, lhs1), (xc0, xc1)
    groups = cp // LANES
    per = LANES // cpad

    barrier = pltpu.get_barrier_semaphore()

    def greet(o, carry):
        pl.semaphore_signal(barrier, inc=1, device_id={"ctx": lax.rem(me + o, n)})
        return carry

    lax.fori_loop(1, n, greet, 0)

    loads = [
        pltpu.make_async_copy(src, dst, in_sem.at[i])
        for i, (src, dst) in enumerate((
            (q_hbm, xin.at[0]), (k_hbm, xin.at[1]), (v_hbm, xin.at[2]),
            (taps_hbm, tin), (filt_hbm, filt),
        ))
    ]
    for i in (1, 2, 3, 0, 4):
        loads[i].start()

    eye = unit(False)
    flip = unit(True)
    channels = n * cblk
    held = 8 + channels
    for half in range(2):
        xc[half][:, 0:n, :] = jnp.zeros((2, n, LANES), F32)
    taps[...] = jnp.zeros((2, 3, 8, cp), F32)
    alt[...] = jnp.zeros((3, 8, cp), F32)
    for a in range(3):
        xf[a, 0:8, :] = jnp.zeros((8, LANES), F32)
        xf[a, held : held + 16, :] = jnp.zeros((16, LANES), F32)

    def turn(a):
        loads[a].wait()
        xf[a, 8:held, :] = xin[a].astype(F32)
        for g in range(groups):
            starts = [8 + (g * per + s) * cblk - low for s in range(per)]
            wide = jnp.concatenate([xf[a, i : i + cpad, :] for i in starts], axis=0).astype(BF16)
            xs[a, 8 : 8 + LANES, g * LANES : (g + 1) * LANES] = to_time_major(eye, wide)

    def halo(a, up):
        if up:
            return pltpu.make_async_remote_copy(
                src_ref=xs.at[a, pl.ds(LANES, 8)], dst_ref=xs.at[a, pl.ds(0, 8)],
                send_sem=hs_sem.at[0, a], recv_sem=hr_sem.at[0, a],
                device_id={"ctx": lax.rem(me + 1, n)},
            )
        return pltpu.make_async_remote_copy(
            src_ref=xs.at[a, pl.ds(8, 8)], dst_ref=xs.at[a, pl.ds(8 + LANES, 8)],
            send_sem=hs_sem.at[1, a], recv_sem=hr_sem.at[1, a],
            device_id={"ctx": lax.rem(me + n - 1, n)},
        )

    @pl.when(me == 0)
    def _():
        xs[:, 0:8, :] = jnp.zeros((3, 8, cp), F32)

    @pl.when(me == n - 1)
    def _():
        xs[:, 8 + LANES : 16 + LANES, :] = jnp.zeros((3, 8, cp), F32)

    def halo_wait(arrays):
        @pl.when(me > 0)
        def _():
            for a in arrays:
                halo(a, True).wait_recv()

        @pl.when(me < n - 1)
        def _():
            for a in arrays:
                halo(a, False).wait_recv()

    def halo_start(arrays):
        @pl.when(me < n - 1)
        def _():
            for a in arrays:
                halo(a, True).start()

        @pl.when(me > 0)
        def _():
            for a in arrays:
                halo(a, False).start()

    turn(1)
    turn(2)
    pl.semaphore_wait(barrier, n - 1)
    halo_start((1, 2))
    turn(0)
    halo_start((0,))
    loads[3].wait()
    for ref, shift in ((taps.at[0], low), (alt, cpad - cblk - low)):
        for b in range(n):
            base = b * cblk - shift
            lo, hi = max(base, 0), min(base + cpad, channels)
            at = b * cpad + lo - base
            ref[:, 0:TAPS, at : at + hi - lo] = tin[:, :, lo:hi]
    turner = unit(True).astype(F32)
    for g in range(groups):
        source = alt[:, :, cp - (g + 1) * LANES : cp - g * LANES].reshape(24, LANES)
        taps[1, :, :, g * LANES : (g + 1) * LANES] = jnp.dot(
            source, turner, precision=lax.Precision.HIGHEST, preferred_element_type=F32
        ).reshape(3, 8, LANES)
    loads[4].wait()
    for d in range(n):
        h32[d] = filt[:, d * LANES : (d + 1) * LANES].astype(F32)

    halo_wait((1, 2))
    for g in range(groups):
        ls = slice(g * LANES, (g + 1) * LANES)
        pa = (short_sum(xs, taps, 0, 1, ls) * short_sum(xs, taps, 0, 2, ls)).astype(BF16)
        pb = (short_sum(xs, taps, 1, 1, ls) * short_sum(xs, taps, 1, 2, ls)).astype(BF16)
        pa = to_channel_major(pa, eye).astype(BF16)
        pb = to_channel_major(pb, flip).astype(BF16)
        for s in range(per):
            block = g * per + s
            for m in range(nch):
                part = slice(s * cpad + m * rows, s * cpad + (m + 1) * rows)
                snd[m, block, 0] = pa[part]
                snd[nch - 1 - m, n - 1 - block, 1] = pb[part]

    def data_copy(m, dest, slot):
        return pltpu.make_async_remote_copy(
            src_ref=snd.at[m, dest], dst_ref=rcv.at[m, slot],
            send_sem=s_sem.at[m], recv_sem=r_sem.at[m],
            device_id={"ctx": dest},
        )

    def back_copy(m, dest, slot):
        return pltpu.make_async_remote_copy(
            src_ref=osnd.at[m, dest], dst_ref=orcv.at[m, slot],
            send_sem=os_sem.at[m], recv_sem=or_sem.at[m],
            device_id={"ctx": dest},
        )

    def all_of(m, src, dst, send_sem, recv_sem):
        return pltpu.make_async_remote_copy(
            src_ref=src.at[m, pl.ds(0, n - 1)], dst_ref=dst.at[m, pl.ds(0, n - 1)],
            send_sem=send_sem.at[m], recv_sem=recv_sem.at[m],
            device_id={"ctx": lax.rem(me + 1, n)},
        )

    def all_data(m):
        return all_of(m, snd, rcv, s_sem, r_sem)

    def all_back(m):
        return all_of(m, osnd, orcv, os_sem, or_sem)

    def each_peer(act):
        def step(o, carry):
            act(lax.rem(me + o, n))
            return carry

        lax.fori_loop(1, n, step, 0)

    for m in range(nch):
        each_peer(lambda peer: data_copy(m, peer, me).start())

    halo_wait((0,))
    for g in range(groups):
        ls = slice(g * LANES, (g + 1) * LANES)
        qmix[0, :, ls] = short_sum(xs, taps, 0, 0, ls)
        qmix[1, :, ls] = short_sum(xs, taps, 1, 0, ls)

    row_id = lax.broadcasted_iota(jnp.int32, (LANES, LANES), 0)
    col_id = lax.broadcasted_iota(jnp.int32, (LANES, LANES), 1)
    causal = col_id >= row_id

    for m in range(nch):
        all_data(m).wait_recv()
        rcv[m, me] = snd[m, me]

        def widen(src, carry):
            at = pl.multiple_of(src * rows, rows)
            xfa[pl.ds(at, rows), :] = rcv[m, src, 0].astype(F32)
            at = pl.multiple_of((n - 1 - src) * rows, rows)
            xfb[pl.ds(at, rows), :] = rcv[m, src, 1].astype(F32)
            return carry

        lax.fori_loop(0, n, widen, 0, unroll=4)

        first = max(m * rows, low)
        last = min((m + 1) * rows, low + cblk)

        count = last - first

        def build(p, half):
            row_a = p - m * rows
            row_b = 2 * low + cblk - 1 - p - (nch - 1 - m) * rows
            row_h = p - low
            line_x = xc[half]
            line_x[0, n : 2 * n, :] = xfa[pl.ds(row_a, n, stride=rows), :]
            line_x[1, n : 2 * n, :] = xfb[pl.ds(row_b, n, stride=rows), :]

            def fill(d, before):
                at = d * LANES
                if not isinstance(d, int):
                    at = pl.multiple_of(at, LANES)
                line = h32[d, pl.ds(row_h, 1), :]
                turned = pltpu.roll(
                    jnp.broadcast_to(line, (LANES, LANES)), 0, 1, stride=1, stride_axis=0
                )
                toep[half][pl.ds(at, LANES), :] = jnp.where(causal, turned, before).astype(BF16)
                xa = line_x[0, pl.ds(n - d, n), :]
                xb = line_x[1, pl.ds(n - d, n), :]
                lhs[half][:, pl.ds(at, LANES)] = jnp.concatenate([xa, xb], axis=0).astype(BF16)
                return turned

            start = jnp.zeros((LANES, LANES), F32)
            if n <= 16:
                for d in range(n):
                    start = fill(d, start)
            else:
                lax.fori_loop(0, n, fill, start)

        def apply(p, half):
            row_a = p - m * rows
            row_b = 2 * low + cblk - 1 - p - (nch - 1 - m) * rows
            y = jnp.dot(lhs[half][...], toep[half][...], preferred_element_type=F32)
            ya[pl.ds(row_a, n, stride=rows), :] = y[:n]
            yb[pl.ds(row_b, n, stride=rows), :] = y[n:]

        def pair(i, carry):
            build(first + 2 * i + 1, 1)
            apply(first + 2 * i, 0)
            build(first + lax.rem(2 * i + 2, count), 0)
            apply(first + 2 * i + 1, 1)
            return carry

        build(first, 0)
        lax.fori_loop(0, count // 2, pair, 0)
        if count % 2:
            apply(last - 1, 0)

        def narrow(dest, carry):
            at = pl.multiple_of(dest * rows, rows)
            osnd[m, dest, 0] = ya[pl.ds(at, rows), :].astype(BF16)
            at = pl.multiple_of((n - 1 - dest) * rows, rows)
            osnd[m, dest, 1] = yb[pl.ds(at, rows), :].astype(BF16)
            return carry

        lax.fori_loop(0, n, narrow, 0, unroll=4)
        each_peer(lambda peer: back_copy(m, peer, me).start())
        orcv[m, me] = osnd[m, me]

    for m in range(nch):
        all_back(m).wait_recv()

    for g in range(groups):
        ls = slice(g * LANES, (g + 1) * LANES)
        blocks = [g * per + s for s in range(per)]
        ma = jnp.concatenate([orcv[m, b, 0] for b in blocks for m in range(nch)], axis=0)
        mb = jnp.concatenate(
            [orcv[nch - 1 - m, n - 1 - b, 1] for b in blocks for m in range(nch)], axis=0
        )
        mixed = qmix[0, :, ls] * to_time_major(eye, ma) + qmix[1, :, ls] * to_time_major(flip, mb)
        mixed = to_channel_major(mixed.astype(BF16), eye)
        for s, b in enumerate(blocks):
            part = mixed[s * cpad + low : s * cpad + low + cblk]
            xf[0, 8 + b * cblk : 8 + (b + 1) * cblk, :] = part
    out[...] = xf[0, 8:held, :].astype(BF16)

    for m in range(nch):
        all_data(m).wait_send()
        all_back(m).wait_send()

    @pl.when(me < n - 1)
    def _():
        for a in range(3):
            halo(a, True).wait_send()

    @pl.when(me > 0)
    def _():
        for a in range(3):
            halo(a, False).wait_send()


def on_device(queries, key_rows, value_rows, short_taps, long_filter):
    n = lax.axis_size("ctx")
    channels, tokens = queries.shape
    cblk, length = long_filter.shape
    cpad, low, rows = dims_of(cblk)
    nch = cpad // rows
    cp = n * cpad
    taps = jnp.swapaxes(short_taps, 1, 2)
    hbm = pl.BlockSpec(memory_space=pltpu.MemorySpace.HBM)
    vmem = pl.BlockSpec(memory_space=pltpu.VMEM)
    dma = pltpu.SemaphoreType.DMA
    return pl.pallas_call(
        functools.partial(kernel, n, cblk),
        out_shape=jax.ShapeDtypeStruct((channels, tokens), BF16),
        in_specs=[hbm] * 5,
        out_specs=vmem,
        scratch_shapes=[
            pltpu.VMEM((3, channels, tokens), BF16),
            pltpu.VMEM((3, TAPS, channels), F32),
            pltpu.VMEM((cblk, length), BF16),
            dma((5,)),
            pltpu.VMEM((3, 8, cp), F32),
            pltpu.VMEM((2, 3, 8, cp), F32),
            pltpu.VMEM((3, channels + 24, LANES), F32),
            pltpu.VMEM((3, LANES + 16, cp), F32),
            pltpu.VMEM((2, LANES, cp), F32),
            pltpu.VMEM((nch, n, 2, rows, LANES), BF16),
            pltpu.VMEM((nch, n, 2, rows, LANES), BF16),
            pltpu.VMEM((nch, n, 2, rows, LANES), BF16),
            pltpu.VMEM((nch, n, 2, rows, LANES), BF16),
            pltpu.VMEM((n, cblk, LANES), F32),
            pltpu.VMEM((n * rows, LANES), F32),
            pltpu.VMEM((n * rows, LANES), F32),
            pltpu.VMEM((n * rows, LANES), F32),
            pltpu.VMEM((n * rows, LANES), F32),
            pltpu.VMEM((length, LANES), BF16),
            pltpu.VMEM((length, LANES), BF16),
            pltpu.VMEM((2 * n, length), BF16),
            pltpu.VMEM((2 * n, length), BF16),
            pltpu.VMEM((2, 2 * n, LANES), F32),
            pltpu.VMEM((2, 2 * n, LANES), F32),
            dma((2, 3)),
            dma((2, 3)),
            dma((nch,)),
            dma((nch,)),
            dma((nch,)),
            dma((nch,)),
        ],
        compiler_params=pltpu.CompilerParams(
            collective_id=0, has_side_effects=True, vmem_limit_bytes=62 * 1024 * 1024
        ),
    )(queries, key_rows, value_rows, taps, long_filter)


def solution(mesh):
    placed = (
        P(None, ("grp", "ctx")),
        P(None, ("grp", "ctx")),
        P(None, ("grp", "ctx")),
        P(),
        P("ctx", None),
    )
    return jax.shard_map(
        on_device, mesh=mesh, in_specs=placed, out_specs=P(None, ("grp", "ctx")), check_vma=False
    )
```

```python
import functools

import jax
import jax.numpy as jnp
from jax import lax
from jax.experimental import pallas as pl
from jax.experimental.pallas import tpu as pltpu
from jax.sharding import PartitionSpec as P

TAPS = 7
LANES = 128
F32 = jnp.float32
BF16 = jnp.bfloat16


def dims_of(cblk):
    cpad = -(-cblk // 16) * 16
    low = (cpad - cblk) // 2
    rows = 16 if cpad % 16 == 0 and 2 * low + cblk == cpad else cpad
    return cpad, low, rows


def unit(flip):
    i = lax.broadcasted_iota(jnp.int32, (LANES, LANES), 0)
    j = lax.broadcasted_iota(jnp.int32, (LANES, LANES), 1)
    j = LANES - 1 - j if flip else j
    return (i == j).astype(F32).astype(BF16)


def to_time_major(mat, x):
    return lax.dot_general(mat, x, (((1,), (1,)), ((), ())), preferred_element_type=F32)


def to_channel_major(x, mat):
    return lax.dot_general(x, mat, (((0,), (0,)), ((), ())), preferred_element_type=F32)


def short_sum(xs, taps, way, which, lanes):
    total = None
    for j in range(TAPS):
        start = 8 - j if way == 0 else 8 + j
        term = taps[way, which, j : j + 1, lanes] * xs[which, start : start + LANES, lanes]
        total = term if total is None else total + term
    return total


def kernel(
    n, cblk, q_hbm, k_hbm, v_hbm, taps_hbm, filt_hbm, out,
    xin, tin, filt, in_sem, alt, taps, xf, xs, qmix, snd, rcv, osnd, orcv, h32, xfa, xfb, ya, yb, toep0, toep1, lhs0, lhs1, xc0, xc1,
    hs_sem, hr_sem, s_sem, r_sem, os_sem, or_sem,
):
    cpad, low, rows = dims_of(cblk)
    nch = cpad // rows
    cp = n * cpad
    me = lax.axis_index("ctx")
    toep, lhs, xc = (toep0, toep1), (lhs0, lhs1), (xc0, xc1)
    groups = cp // LANES
    per = LANES // cpad

    barrier = pltpu.get_barrier_semaphore()

    def greet(o, carry):
        pl.semaphore_signal(barrier, inc=1, device_id={"ctx": lax.rem(me + o, n)})
        return carry

    lax.fori_loop(1, n, greet, 0)

    loads = [
        pltpu.make_async_copy(src, dst, in_sem.at[i])
        for i, (src, dst) in enumerate((
            (q_hbm, xin.at[0]), (k_hbm, xin.at[1]), (v_hbm, xin.at[2]),
            (taps_hbm, tin), (filt_hbm, filt),
        ))
    ]
    for i in (1, 2, 3, 0, 4):
        loads[i].start()

    eye = unit(False)
    flip = unit(True)
    channels = n * cblk
    held = 8 + channels
    for half in range(2):
        xc[half][:, 0:n, :] = jnp.zeros((2, n, LANES), F32)
    taps[...] = jnp.zeros((2, 3, 8, cp), F32)
    alt[...] = jnp.zeros((3, 8, cp), F32)
    for a in range(3):
        xf[a, 0:8, :] = jnp.zeros((8, LANES), F32)
        xf[a, held : held + 16, :] = jnp.zeros((16, LANES), F32)

    def turn(a):
        loads[a].wait()
        xf[a, 8:held, :] = xin[a].astype(F32)
        for g in range(groups):
            starts = [8 + (g * per + s) * cblk - low for s in range(per)]
            wide = jnp.concatenate([xf[a, i : i + cpad, :] for i in starts], axis=0).astype(BF16)
            xs[a, 8 : 8 + LANES, g * LANES : (g + 1) * LANES] = to_time_major(eye, wide)

    def halo(a, up):
        if up:
            return pltpu.make_async_remote_copy(
                src_ref=xs.at[a, pl.ds(LANES, 8)], dst_ref=xs.at[a, pl.ds(0, 8)],
                send_sem=hs_sem.at[0, a], recv_sem=hr_sem.at[0, a],
                device_id={"ctx": lax.rem(me + 1, n)},
            )
        return pltpu.make_async_remote_copy(
            src_ref=xs.at[a, pl.ds(8, 8)], dst_ref=xs.at[a, pl.ds(8 + LANES, 8)],
            send_sem=hs_sem.at[1, a], recv_sem=hr_sem.at[1, a],
            device_id={"ctx": lax.rem(me + n - 1, n)},
        )

    @pl.when(me == 0)
    def _():
        xs[:, 0:8, :] = jnp.zeros((3, 8, cp), F32)

    @pl.when(me == n - 1)
    def _():
        xs[:, 8 + LANES : 16 + LANES, :] = jnp.zeros((3, 8, cp), F32)

    def halo_wait(arrays):
        @pl.when(me > 0)
        def _():
            for a in arrays:
                halo(a, True).wait_recv()

        @pl.when(me < n - 1)
        def _():
            for a in arrays:
                halo(a, False).wait_recv()

    def halo_start(arrays):
        @pl.when(me < n - 1)
        def _():
            for a in arrays:
                halo(a, True).start()

        @pl.when(me > 0)
        def _():
            for a in arrays:
                halo(a, False).start()

    turn(1)
    turn(2)
    pl.semaphore_wait(barrier, n - 1)
    halo_start((1, 2))
    turn(0)
    halo_start((0,))
    loads[3].wait()
    for ref, shift in ((taps.at[0], low), (alt, cpad - cblk - low)):
        for b in range(n):
            base = b * cblk - shift
            lo, hi = max(base, 0), min(base + cpad, channels)
            at = b * cpad + lo - base
            ref[:, 0:TAPS, at : at + hi - lo] = tin[:, :, lo:hi]
    turner = unit(True).astype(F32)
    for g in range(groups):
        source = alt[:, :, cp - (g + 1) * LANES : cp - g * LANES].reshape(24, LANES)
        taps[1, :, :, g * LANES : (g + 1) * LANES] = jnp.dot(
            source, turner, precision=lax.Precision.HIGHEST, preferred_element_type=F32
        ).reshape(3, 8, LANES)
    loads[4].wait()
    for d in range(n):
        h32[d] = filt[:, d * LANES : (d + 1) * LANES].astype(F32)

    halo_wait((1, 2))
    for g in range(groups):
        ls = slice(g * LANES, (g + 1) * LANES)
        pa = (short_sum(xs, taps, 0, 1, ls) * short_sum(xs, taps, 0, 2, ls)).astype(BF16)
        pb = (short_sum(xs, taps, 1, 1, ls) * short_sum(xs, taps, 1, 2, ls)).astype(BF16)
        pa = to_channel_major(pa, eye).astype(BF16)
        pb = to_channel_major(pb, flip).astype(BF16)
        for s in range(per):
            block = g * per + s
            for m in range(nch):
                part = slice(s * cpad + m * rows, s * cpad + (m + 1) * rows)
                snd[m, block, 0] = pa[part]
                snd[nch - 1 - m, n - 1 - block, 1] = pb[part]

    def data_copy(m, dest, slot):
        return pltpu.make_async_remote_copy(
            src_ref=snd.at[m, dest], dst_ref=rcv.at[m, slot],
            send_sem=s_sem.at[m], recv_sem=r_sem.at[m],
            device_id={"ctx": dest},
        )

    def back_copy(m, dest, slot):
        return pltpu.make_async_remote_copy(
            src_ref=osnd.at[m, dest], dst_ref=orcv.at[m, slot],
            send_sem=os_sem.at[m], recv_sem=or_sem.at[m],
            device_id={"ctx": dest},
        )

    def all_of(m, src, dst, send_sem, recv_sem):
        return pltpu.make_async_remote_copy(
            src_ref=src.at[m, pl.ds(0, n - 1)], dst_ref=dst.at[m, pl.ds(0, n - 1)],
            send_sem=send_sem.at[m], recv_sem=recv_sem.at[m],
            device_id={"ctx": lax.rem(me + 1, n)},
        )

    def all_data(m):
        return all_of(m, snd, rcv, s_sem, r_sem)

    def all_back(m):
        return all_of(m, osnd, orcv, os_sem, or_sem)

    def each_peer(act):
        def step(o, carry):
            act(lax.rem(me + o, n))
            return carry

        lax.fori_loop(1, n, step, 0, unroll=3)

    for m in range(nch):
        each_peer(lambda peer: data_copy(m, peer, me).start())

    halo_wait((0,))
    for g in range(groups):
        ls = slice(g * LANES, (g + 1) * LANES)
        qmix[0, :, ls] = short_sum(xs, taps, 0, 0, ls)
        qmix[1, :, ls] = short_sum(xs, taps, 1, 0, ls)

    row_id = lax.broadcasted_iota(jnp.int32, (LANES, LANES), 0)
    col_id = lax.broadcasted_iota(jnp.int32, (LANES, LANES), 1)
    causal = col_id >= row_id

    for m in range(nch):
        all_data(m).wait_recv()
        rcv[m, me] = snd[m, me]

        def widen(src, carry):
            at = pl.multiple_of(src * rows, rows)
            xfa[pl.ds(at, rows), :] = rcv[m, src, 0].astype(F32)
            at = pl.multiple_of((n - 1 - src) * rows, rows)
            xfb[pl.ds(at, rows), :] = rcv[m, src, 1].astype(F32)
            return carry

        lax.fori_loop(0, n, widen, 0, unroll=8)

        first = max(m * rows, low)
        last = min((m + 1) * rows, low + cblk)

        count = last - first

        def build(p, half):
            row_a = p - m * rows
            row_b = 2 * low + cblk - 1 - p - (nch - 1 - m) * rows
            row_h = p - low
            line_x = xc[half]
            line_x[0, n : 2 * n, :] = xfa[pl.ds(row_a, n, stride=rows), :]
            line_x[1, n : 2 * n, :] = xfb[pl.ds(row_b, n, stride=rows), :]

            def fill(d, before):
                at = d * LANES
                if not isinstance(d, int):
                    at = pl.multiple_of(at, LANES)
                line = h32[d, pl.ds(row_h, 1), :]
                turned = pltpu.roll(
                    jnp.broadcast_to(line, (LANES, LANES)), 0, 1, stride=1, stride_axis=0
                )
                toep[half][pl.ds(at, LANES), :] = jnp.where(causal, turned, before).astype(BF16)
                xa = line_x[0, pl.ds(n - d, n), :]
                xb = line_x[1, pl.ds(n - d, n), :]
                lhs[half][:, pl.ds(at, LANES)] = jnp.concatenate([xa, xb], axis=0).astype(BF16)
                return turned

            start = jnp.zeros((LANES, LANES), F32)
            if n <= 16:
                for d in range(n):
                    start = fill(d, start)
            else:
                lax.fori_loop(0, n, fill, start)

        def apply(p, half):
            row_a = p - m * rows
            row_b = 2 * low + cblk - 1 - p - (nch - 1 - m) * rows
            y = jnp.dot(lhs[half][...], toep[half][...], preferred_element_type=F32)
            ya[pl.ds(row_a, n, stride=rows), :] = y[:n]
            yb[pl.ds(row_b, n, stride=rows), :] = y[n:]

        def pair(i, carry):
            build(first + 2 * i + 1, 1)
            apply(first + 2 * i, 0)
            build(first + lax.rem(2 * i + 2, count), 0)
            apply(first + 2 * i + 1, 1)
            return carry

        build(first, 0)
        lax.fori_loop(0, count // 2, pair, 0)
        if count % 2:
            apply(last - 1, 0)

        def narrow(dest, carry):
            at = pl.multiple_of(dest * rows, rows)
            osnd[m, dest, 0] = ya[pl.ds(at, rows), :].astype(BF16)
            at = pl.multiple_of((n - 1 - dest) * rows, rows)
            osnd[m, dest, 1] = yb[pl.ds(at, rows), :].astype(BF16)
            return carry

        lax.fori_loop(0, n, narrow, 0, unroll=8)
        each_peer(lambda peer: back_copy(m, peer, me).start())
        orcv[m, me] = osnd[m, me]

    for m in range(nch):
        all_back(m).wait_recv()

    for g in range(groups):
        ls = slice(g * LANES, (g + 1) * LANES)
        blocks = [g * per + s for s in range(per)]
        ma = jnp.concatenate([orcv[m, b, 0] for b in blocks for m in range(nch)], axis=0)
        mb = jnp.concatenate(
            [orcv[nch - 1 - m, n - 1 - b, 1] for b in blocks for m in range(nch)], axis=0
        )
        mixed = qmix[0, :, ls] * to_time_major(eye, ma) + qmix[1, :, ls] * to_time_major(flip, mb)
        mixed = to_channel_major(mixed.astype(BF16), eye)
        for s, b in enumerate(blocks):
            part = mixed[s * cpad + low : s * cpad + low + cblk]
            xf[0, 8 + b * cblk : 8 + (b + 1) * cblk, :] = part
    out[...] = xf[0, 8:held, :].astype(BF16)

    for m in range(nch):
        all_data(m).wait_send()
        all_back(m).wait_send()

    @pl.when(me < n - 1)
    def _():
        for a in range(3):
            halo(a, True).wait_send()

    @pl.when(me > 0)
    def _():
        for a in range(3):
            halo(a, False).wait_send()


def on_device(queries, key_rows, value_rows, short_taps, long_filter):
    n = lax.axis_size("ctx")
    channels, tokens = queries.shape
    cblk, length = long_filter.shape
    cpad, low, rows = dims_of(cblk)
    nch = cpad // rows
    cp = n * cpad
    taps = jnp.swapaxes(short_taps, 1, 2)
    hbm = pl.BlockSpec(memory_space=pltpu.MemorySpace.HBM)
    vmem = pl.BlockSpec(memory_space=pltpu.VMEM)
    dma = pltpu.SemaphoreType.DMA
    return pl.pallas_call(
        functools.partial(kernel, n, cblk),
        out_shape=jax.ShapeDtypeStruct((channels, tokens), BF16),
        in_specs=[hbm] * 5,
        out_specs=vmem,
        scratch_shapes=[
            pltpu.VMEM((3, channels, tokens), BF16),
            pltpu.VMEM((3, TAPS, channels), F32),
            pltpu.VMEM((cblk, length), BF16),
            dma((5,)),
            pltpu.VMEM((3, 8, cp), F32),
            pltpu.VMEM((2, 3, 8, cp), F32),
            pltpu.VMEM((3, channels + 24, LANES), F32),
            pltpu.VMEM((3, LANES + 16, cp), F32),
            pltpu.VMEM((2, LANES, cp), F32),
            pltpu.VMEM((nch, n, 2, rows, LANES), BF16),
            pltpu.VMEM((nch, n, 2, rows, LANES), BF16),
            pltpu.VMEM((nch, n, 2, rows, LANES), BF16),
            pltpu.VMEM((nch, n, 2, rows, LANES), BF16),
            pltpu.VMEM((n, cblk, LANES), F32),
            pltpu.VMEM((n * rows, LANES), F32),
            pltpu.VMEM((n * rows, LANES), F32),
            pltpu.VMEM((n * rows, LANES), F32),
            pltpu.VMEM((n * rows, LANES), F32),
            pltpu.VMEM((length, LANES), BF16),
            pltpu.VMEM((length, LANES), BF16),
            pltpu.VMEM((2 * n, length), BF16),
            pltpu.VMEM((2 * n, length), BF16),
            pltpu.VMEM((2, 2 * n, LANES), F32),
            pltpu.VMEM((2, 2 * n, LANES), F32),
            dma((2, 3)),
            dma((2, 3)),
            dma((nch,)),
            dma((nch,)),
            dma((nch,)),
            dma((nch,)),
        ],
        compiler_params=pltpu.CompilerParams(
            collective_id=0, has_side_effects=True, vmem_limit_bytes=62 * 1024 * 1024
        ),
    )(queries, key_rows, value_rows, taps, long_filter)


def solution(mesh):
    placed = (
        P(None, ("grp", "ctx")),
        P(None, ("grp", "ctx")),
        P(None, ("grp", "ctx")),
        P(),
        P("ctx", None),
    )
    return jax.shard_map(
        on_device, mesh=mesh, in_specs=placed, out_specs=P(None, ("grp", "ctx")), check_vma=False
    )
```
